256 devices in a mesh: row: 4 (over z_hi, core), real: 64 (over x, y, z_lo).
Axes of the slice: x: 4, y: 4, z: 8 (z_hi: 2, z_lo: 4; z = z_hi * 4 + z_lo), core: 2. Of those that a mesh axis runs over, the one named last changes fastest.
Arguments:
- right_sides: float32 [10, 4, 256, 32768], P(None, 'row', None, 'real'), may hold values from -8 to 8
- factor: float32 [10, 4, 256, 1024], P(None, 'row', None, 'real'), may hold values from -1 to 2, as said below
Outputs:
- updated: float32 [10, 4, 256, 32768], P(None, 'row', None, 'real')
The draws below stay inside these ranges and needn't reach their ends.
Inputs may be any that keep to these rules, and one draw needn't show every extreme that they name: factor is lower triangular in global row and column order (entries with column above the global row are 0), with diagonal entries from 1 to 2.
All inputs are finite; a program needn't handle non-finite values.
Results may differ from the reference program's by a relative error of at most 0.0001.
Values sent between devices are 32-bit elements; how exact they have to be, the bound alone decides.
A program may use at most 128 MiB of HBM per device.

```python
import math
import jax
import jax.numpy as jnp
from jax import lax

PANEL = 256
BLK_DEV = 10
WINDOW = 1024
ACTIVE = 10240
NRHS = 32768
N_ROW = 4


def draw_factor(key, part):
    first_key, second_key = jax.random.split(key, 2)
    full_shape = (BLK_DEV, N_ROW, PANEL, WINDOW)
    coupling = jax.random.normal(first_key, full_shape, jnp.float32)
    coupling = coupling / math.sqrt(WINDOW)
    diagonal_vals = jax.random.uniform(second_key, (BLK_DEV, N_ROW, PANEL, 1), jnp.float32, 1.0, 2.0)
    block_index = jnp.arange(BLK_DEV)[:, None] * N_ROW + jnp.arange(N_ROW)[None, :]
    row_index = block_index[:, :, None, None] * PANEL + jnp.arange(PANEL)[None, None, :, None]
    col_index = jnp.arange(WINDOW)[None, None, None, :]
    below_mask = col_index < row_index
    on_diagonal = col_index == row_index
    return jnp.where(below_mask, coupling, 0.0) + jnp.where(on_diagonal, diagonal_vals, 0.0)


def levels(own_key, extent, cuts, least, largest):
    factor_of = 1.0
    for position, blocks in cuts:
        heights = jax.random.uniform(jax.random.fold_in(jax.random.fold_in(own_key, 6), position), (blocks,), jnp.float32, least / len(cuts), largest / len(cuts))
        factor_of = factor_of * jnp.repeat(jnp.exp(heights), extent[position] // blocks).reshape((-1,) + (1,) * (len(extent) - 1 - position))
    return factor_of


def noise(own_key, dims, deviation, reach, cuts=(), dtype=jnp.bfloat16):
    gain = levels(own_key, dims, cuts, -0.22, 0.18) if cuts else 1.0
    array = jax.random.normal(own_key, dims, jnp.float32) * deviation * gain
    return jnp.minimum(jnp.maximum(array, -reach), reach).astype(dtype)


def setup_inputs(seed: int = 0) -> dict:
    streams_of = jax.random.split(jax.random.key(seed), 3)
    return {
        "right_sides": noise(streams_of[0], (BLK_DEV, N_ROW, PANEL, NRHS), 1.0, 8.0, ((1, 4), (3, 64)), jnp.float32),
        "factor": draw_factor(jax.random.fold_in(streams_of[2], 71), 0),
    }


def reference(right_sides, factor):
    working = right_sides.reshape(ACTIVE, NRHS)
    matrix = factor.reshape(ACTIVE, WINDOW)
    for panel_index in range(N_ROW):
        lower_edge = panel_index * PANEL
        upper_edge = lower_edge + PANEL
        diagonal_block = matrix[lower_edge:upper_edge, lower_edge:upper_edge]
        answer = lax.linalg.triangular_solve(diagonal_block, working[lower_edge:upper_edge], left_side=True, lower=True)
        below = working[upper_edge:] - jnp.dot(matrix[upper_edge:, lower_edge:upper_edge], answer, precision=lax.Precision.HIGHEST)
        working = jnp.concatenate([working[:lower_edge], answer, below], axis=0)
    return working.reshape(BLK_DEV, N_ROW, PANEL, NRHS)
```

```python
import jax
import jax.numpy as jnp
from jax import lax
from jax.experimental import pallas as pl
from jax.experimental.pallas import tpu as pltpu
from jax.sharding import PartitionSpec as P

MESH = pl.DeviceIdType.MESH
PIECES = 11
SLOTS = 13
HI = lax.Precision.HIGHEST


def gather_kernel(ft, rhs, lt, bh, rsem, zsem, zsend, ssem, bsem, bsend, xsem, xsend):
    row = lax.axis_index("row")
    real = lax.axis_index("real")
    zh, core = row // 2, row % 2
    x0, y0, z0 = real // 16, (real // 4) % 4, real % 4
    other = (1 - zh) * 2 + core
    sibling = zh * 2 + (1 - core)

    def place(x, y, z):
        return (x % 4) * 16 + (y % 4) * 4 + z

    near = [(row, place(x0 + d, y0, z0)) for d in (1, 3)]
    near += [(row, place(x0, y0 + d, z0)) for d in (1, 3)]
    near += [(row, place(x0, y0, (z0 + d) % 4)) for d in (1, 2, 3)]
    near += [(other, place(x0, y0, z)) for z in range(4)]
    near += [(sibling, real)]
    barrier = pltpu.get_barrier_semaphore()
    for device in near:
        pl.semaphore_signal(barrier, inc=1, device_id=device, device_id_type=MESH)
    pl.semaphore_wait(barrier, len(near))

    def chunk(p, h):
        return lt.at[p, h, x0 * 4 + y0, pl.ds(16 * z0, 16)]

    def own(block, h):
        return ft.at[block, :, pl.ds(128 * h, 128)]

    def scatter_z(p, block):
        for h in (0, 1):
            pltpu.make_async_copy(own(block, h), chunk(p, h), zsem.at[p, h]).start()
            for d in (1, 2, 3):
                pltpu.make_async_remote_copy(
                    own(block, h), chunk(p, h), zsend.at[p, h], zsem.at[p, h],
                    device_id=(row, place(x0, y0, (z0 + d) % 4)), device_id_type=MESH,
                ).start()

    scatter_z(0, 0)
    for h in (0, 1):
        for z in range(4):
            pltpu.make_async_remote_copy(
                own(0, h), chunk(1, h), zsend.at[1, h], zsem.at[1, h],
                device_id=(other, place(x0, y0, z)), device_id_type=MESH,
            ).start()
    half_copy = pltpu.make_async_remote_copy(
        rhs.at[0], bh.at[0], bsend.at[0], bsem.at[0], device_id=(other, real), device_id_type=MESH
    )
    half_copy.start()
    core_copy = pltpu.make_async_remote_copy(
        rhs.at[0], bh.at[1], bsend.at[1], bsem.at[1], device_id=(sibling, real), device_id_type=MESH
    )
    core_copy.start()

    @pl.loop(2, PIECES)
    def _(p):
        scatter_z(p, p - 1)

    def slab(p, h, a, b, half=None):
        x, y = ((x0 + a) % 4, (y0 + b) % 4) if h == 0 else ((x0 + b) % 4, (y0 + a) % 4)
        if half is None:
            return lt.at[p, h, x * 4 + y]
        return lt.at[p, h, x * 4 + y, pl.ds(32 * half, 32)]

    def target(h, first, step):
        if (h == 0) == first:
            return (row, place(x0 + step, y0, z0))
        return (row, place(x0, y0 + step, z0))

    def send(p, h, a, b, first, step, k, half=None):
        ref = slab(p, h, a, b, half)
        pltpu.make_async_remote_copy(
            ref, ref, ssem.at[p, h], rsem.at[p, h, k],
            device_id=target(h, first, step), device_id_type=MESH,
        ).start()

    def await_rows(p, h, k, slabs=1):
        ref = lt.at[p, h, pl.ds(0, slabs)]
        pltpu.make_async_copy(ref, ref, rsem.at[p, h, k]).wait()

    def phase1(p):
        for h in (0, 1):
            ref = lt.at[p, h, 0]
            pltpu.make_async_copy(ref, ref, zsem.at[p, h]).wait()
            send(p, h, 0, 0, True, 1, 1)
            send(p, h, 0, 0, True, 3, 2)
            send(p, h, 0, 0, False, 1, 4)
            send(p, h, 0, 0, False, 3, 5)

    def phase2(p):
        for h in (0, 1):
            await_rows(p, h, 1)
            send(p, h, 3, 0, True, 1, 3, 0)
            send(p, h, 3, 0, False, 1, 7)
            send(p, h, 3, 0, False, 3, 8)
        for h in (0, 1):
            await_rows(p, h, 2)
            send(p, h, 1, 0, True, 3, 3, 1)
            send(p, h, 1, 0, False, 1, 7)
            send(p, h, 1, 0, False, 3, 8)
        for h in (0, 1):
            await_rows(p, h, 4)
            send(p, h, 0, 3, False, 1, 6, 0)
            await_rows(p, h, 5)
            send(p, h, 0, 1, False, 3, 6, 1)

    def phase3(p):
        for h in (0, 1):
            await_rows(p, h, 3)
            send(p, h, 2, 0, False, 1, 10)
            send(p, h, 2, 0, False, 3, 11)
        for h in (0, 1):
            await_rows(p, h, 7, 2)
            send(p, h, 3, 3, False, 1, 9, 0)
            send(p, h, 1, 3, False, 1, 9, 0)
            await_rows(p, h, 8, 2)
            send(p, h, 3, 1, False, 3, 9, 1)
            send(p, h, 1, 1, False, 3, 9, 1)

    def phase4(p):
        for h in (0, 1):
            await_rows(p, h, 10)
            send(p, h, 2, 3, False, 1, 12, 0)
            await_rows(p, h, 11)
            send(p, h, 2, 1, False, 3, 12, 1)

    def finish(p):
        for h in (0, 1):
            await_rows(p, h, 6)
            await_rows(p, h, 9, 2)
            await_rows(p, h, 12)

    @pl.loop(0, PIECES + 5)
    def _(t):
        pl.when(t < PIECES)(lambda: phase1(t))
        pl.when((t >= 2) & (t < PIECES + 2))(lambda: phase2(t - 2))
        pl.when((t >= 3) & (t < PIECES + 3))(lambda: phase3(t - 3))
        pl.when((t >= 4) & (t < PIECES + 4))(lambda: phase4(t - 4))
        pl.when(t >= 5)(lambda: finish(t - 5))

        @pl.when(t == 6)
        def _():
            for p in (0, 1):
                pltpu.make_async_remote_copy(
                    lt.at[p], lt.at[PIECES + p], xsend.at[p], xsem.at[p],
                    device_id=(sibling, real), device_id_type=MESH,
                ).start()

    half_copy.wait()
    core_copy.wait()
    last = pltpu.make_async_remote_copy(
        bh.at[0], bh.at[2], bsend.at[2], bsem.at[2], device_id=(sibling, real), device_id_type=MESH
    )
    last.start()
    last.wait()
    for p in (0, 1):
        pltpu.make_async_remote_copy(
            lt.at[p], lt.at[PIECES + p], xsend.at[p], xsem.at[p],
            device_id=(sibling, real), device_id_type=MESH,
        ).wait()

    @pl.loop(0, PIECES)
    def _(p):
        for h in (0, 1):
            part = lt.at[p, h, 0, pl.ds(0, 48)]
            pltpu.make_async_copy(part, part, zsend.at[p, h]).wait()
            part = lt.at[p, h, pl.ds(0, 15)]
            pltpu.make_async_copy(part, part, ssem.at[p, h]).wait()

    for h in (0, 1):
        part = lt.at[1, h, 0, pl.ds(0, 16)]
        pltpu.make_async_copy(part, part, zsend.at[1, h]).wait()


def gather(ft, rhs):
    dma = pltpu.SemaphoreType.DMA
    anywhere = pl.BlockSpec(memory_space=pl.ANY)
    return pl.pallas_call(
        gather_kernel,
        out_shape=(
            jax.ShapeDtypeStruct((SLOTS, 2, 16, 64, 128), jnp.float32),
            jax.ShapeDtypeStruct((3, 256, 512), jnp.float32),
        ),
        in_specs=[anywhere, anywhere],
        out_specs=(anywhere, anywhere),
        scratch_shapes=[
            dma((PIECES, 2, 13)), dma((PIECES, 2)), dma((PIECES, 2)), dma((PIECES, 2)),
            dma((3,)), dma((3,)), dma((2,)), dma((2,)),
        ],
        compiler_params=pltpu.CompilerParams(collective_id=0, has_side_effects=True),
        name="gather",
    )(ft, rhs)


def dot_t(a, b, precision=None):
    return lax.dot_general(
        a, b, (((0,), (0,)), ((), ())), precision=precision, preferred_element_type=jnp.float32
    )


def split(value):
    high = value.astype(jnp.bfloat16)
    return high, (value - high.astype(jnp.float32)).astype(jnp.bfloat16)


def invert(upper):
    r = lax.broadcasted_iota(jnp.int32, (128, 128), 0)
    c = lax.broadcasted_iota(jnp.int32, (128, 128), 1)
    diagonal = jnp.where(r == c, upper, 0.0)
    x = jnp.where(r == c, 1.0 / jnp.sum(diagonal, axis=0, keepdims=True), 0.0)
    size = 1
    while size < 128:
        cross = jnp.where((c // (2 * size) == r // (2 * size)) & (c // size != r // size) & (c > r), upper, 0.0)
        inner = jnp.dot(x, cross, precision=HI, preferred_element_type=jnp.float32)
        x = x - jnp.dot(inner, x, precision=HI, preferred_element_type=jnp.float32)
        size *= 2
    return x


def solve_kernel(rhs, lt, lt_all, bh, out, head, first, sem, y, yh, yl):
    b = pl.program_id(0)
    row = lax.axis_index("row")
    zh, core = row // 2, row % 2

    @pl.when(b == 0)
    def _():
        copies = []
        for k in range(4):
            kh, kc = k // 2, k % 2
            away = (kh + zh) % 2
            side = (kc + core) % 2
            slot = away + 11 * side
            copies.append(pltpu.make_async_copy(lt_all.at[slot], head.at[k], sem.at[k]))
        for i in range(3):
            copies.append(pltpu.make_async_copy(bh.at[i], first.at[i], sem.at[4 + i]))
        for copy in copies:
            copy.start()
        first[3] = rhs[0]
        for copy in copies:
            copy.wait()
        for k in range(4):
            kh, kc = k // 2, k % 2
            away = (kh + zh) % 2
            side = (kc + core) % 2
            index = jnp.where(away == 1, jnp.where(side == 1, 2, 0), jnp.where(side == 1, 1, 3))
            for h in (0, 1):
                at = 256 * k + 128 * h
                value = first[index, pl.ds(128 * h, 128), :]
                if at:
                    value = value - dot_t(head[k, h, 0:at, :], y[0:at, :], HI)
                x = invert(head[k, h, at : at + 128, :])
                y[at : at + 128, :] = dot_t(x, value, HI)
        high, low = split(y[...])
        yh[...] = high
        yl[...] = low
        out[0] = y[pl.ds(pl.multiple_of(row * 256, 256), 256), :]

    @pl.when(b > 0)
    def _():
        for h in (0, 1):
            high, low = split(lt[0, h])
            update = dot_t(high, yh[...]) + dot_t(high, yl[...]) + dot_t(low, yh[...])
            out[0, 128 * h : 128 * h + 128, :] = rhs[0, 128 * h : 128 * h + 128, :] - update


def solve(rhs, lt, bh):
    anywhere = pl.BlockSpec(memory_space=pl.ANY)
    return pl.pallas_call(
        solve_kernel,
        out_shape=jax.ShapeDtypeStruct((10, 256, 512), jnp.float32),
        grid=(10,),
        in_specs=[
            pl.BlockSpec((1, 256, 512), lambda b: (b, 0, 0)),
            pl.BlockSpec((1, 2, 1024, 128), lambda b: (jnp.maximum(b, 1) + 1, 0, 0, 0)),
            anywhere,
            anywhere,
        ],
        out_specs=pl.BlockSpec((1, 256, 512), lambda b: (b, 0, 0)),
        scratch_shapes=[
            pltpu.VMEM((4, 2, 1024, 128), jnp.float32),
            pltpu.VMEM((4, 256, 512), jnp.float32),
            pltpu.SemaphoreType.DMA((7,)),
            pltpu.VMEM((1024, 512), jnp.float32),
            pltpu.VMEM((1024, 512), jnp.bfloat16),
            pltpu.VMEM((1024, 512), jnp.bfloat16),
        ],
        compiler_params=pltpu.CompilerParams(vmem_limit_bytes=60 * 1024 * 1024),
        name="solve",
    )(rhs, lt, lt, bh)


def body(right_sides, factor):
    rhs = right_sides[:, 0]
    lt, bh = gather(jnp.swapaxes(factor[:, 0], 1, 2), rhs)
    return solve(rhs, lt.reshape(SLOTS, 2, 1024, 128), bh)[:, None]


def solution(mesh):
    placed = (P(None, "row", None, "real"), P(None, "row", None, "real"))
    return jax.shard_map(
        body, mesh=mesh, in_specs=placed, out_specs=P(None, "row", None, "real"), check_vma=False
    )
```

```python
import jax
import jax.numpy as jnp
from jax import lax
from jax.experimental import pallas as pl
from jax.experimental.pallas import tpu as pltpu
from jax.sharding import PartitionSpec as P

MESH = pl.DeviceIdType.MESH
PIECES = 11
SLOTS = 13
AHEAD = 4
RIGHT_FROM, RIGHT_BY = 4, 9
INVERT_OWN, INVERT_SIBLING, SOLVE = 7, 8, 10
HI = lax.Precision.HIGHEST


def dot(a, b, precision=None):
    return jnp.dot(a, b, precision=precision, preferred_element_type=jnp.float32)


def dot_t(a, b, precision=None):
    return lax.dot_general(
        a, b, (((0,), (0,)), ((), ())), precision=precision, preferred_element_type=jnp.float32
    )


def split(value):
    high = value.astype(jnp.bfloat16)
    return high, (value - high.astype(jnp.float32)).astype(jnp.bfloat16)


def product(lt_part, yh, yl):
    high, low = split(lt_part)
    return dot_t(high, yh) + dot_t(high, yl) + dot_t(low, yh)


def invert(uppers):
    r = lax.broadcasted_iota(jnp.int32, (128, 128), 0)
    c = lax.broadcasted_iota(jnp.int32, (128, 128), 1)
    xs = [
        jnp.where(r == c, 1.0 / jnp.sum(jnp.where(r == c, u, 0.0), axis=0, keepdims=True), 0.0)
        for u in uppers
    ]
    size = 1
    while size < 128:
        cross = (c // (2 * size) == r // (2 * size)) & (c // size != r // size) & (c > r)
        inner = [dot(x, jnp.where(cross, u, 0.0), HI) for x, u in zip(xs, uppers)]
        xs = [x - dot(i, x, HI) for x, i in zip(xs, inner)]
        size *= 2
    return xs


def kernel(
    ft, rhs, out, lt, stage, bh, work, xinv, y, yh, yl,
    rsem, zsem, zsend, ssem, stsem, bsem, bsend, xsem, xsend, insem, outsem,
):
    row = lax.axis_index("row")
    real = lax.axis_index("real")
    zh, core = row // 2, row % 2
    x0, y0, z0 = real // 16, (real // 4) % 4, real % 4
    other = (1 - zh) * 2 + core
    sibling = zh * 2 + (1 - core)

    def place(x, y, z):
        return (x % 4) * 16 + (y % 4) * 4 + z

    near = [(row, place(x0 + d, y0, z0)) for d in (1, 3)]
    near += [(row, place(x0, y0 + d, z0)) for d in (1, 3)]
    near += [(row, place(x0, y0, (z0 + d) % 4)) for d in (1, 2, 3)]
    near += [(other, place(x0, y0, z)) for z in range(4)]
    near += [(sibling, real)]
    barrier = pltpu.get_barrier_semaphore()
    pltpu.make_async_copy(rhs, work, insem.at[0]).start()
    pltpu.make_async_copy(rhs.at[0], bh.at[3], insem.at[1]).start()
    for h in (0, 1):
        pltpu.make_async_copy(ft.at[:, :, pl.ds(128 * h, 128)], stage.at[:, h], stsem.at[h]).start()
    for device in near:
        pl.semaphore_signal(barrier, inc=1, device_id=device, device_id_type=MESH)
    for h in (0, 1):
        pltpu.make_async_copy(ft.at[:, :, pl.ds(128 * h, 128)], stage.at[:, h], stsem.at[h]).wait()
    pl.semaphore_wait(barrier, len(near))

    def chunk(p):
        return lt.at[p, :, x0 * 4 + y0, pl.ds(16 * z0, 16)]

    def scatter_z(p, block):
        for h in (0, 1):
            own = ft.at[block, :, pl.ds(128 * h, 128)]
            mine = lt.at[p, h, x0 * 4 + y0, pl.ds(16 * z0, 16)]
            pltpu.make_async_copy(own, mine, zsem.at[p]).start()
        for d in (1, 2, 3):
            pltpu.make_async_remote_copy(
                stage.at[block], chunk(p), zsend.at[p], zsem.at[p],
                device_id=(row, place(x0, y0, (z0 + d) % 4)), device_id_type=MESH,
            ).start()

    def half_copy(rows):
        return pltpu.make_async_remote_copy(
            rhs.at[0, rows], bh.at[0, rows], bsend.at[0], bsem.at[0],
            device_id=(other, real), device_id_type=MESH,
        )

    scatter_z(0, 0)
    for z in range(4):
        pltpu.make_async_remote_copy(
            stage.at[0], chunk(1), zsend.at[1], zsem.at[1],
            device_id=(other, place(x0, y0, z)), device_id_type=MESH,
        ).start()
    for p in range(2, AHEAD):
        scatter_z(p, p - 1)
    core_copy = pltpu.make_async_remote_copy(
        rhs.at[0], bh.at[1], bsend.at[1], bsem.at[1], device_id=(sibling, real), device_id_type=MESH
    )
    core_copy.start()
    last = pltpu.make_async_remote_copy(
        bh.at[0], bh.at[2], bsend.at[2], bsem.at[2], device_id=(sibling, real), device_id_type=MESH
    )

    def sibling_head(p):
        return pltpu.make_async_remote_copy(
            lt.at[p], lt.at[PIECES + p], xsend.at[p], xsem.at[p],
            device_id=(sibling, real), device_id_type=MESH,
        )

    def slab(p, h, a, b, half=None):
        x, y = ((x0 + a) % 4, (y0 + b) % 4) if h == 0 else ((x0 + b) % 4, (y0 + a) % 4)
        if half is None:
            return lt.at[p, h, x * 4 + y]
        return lt.at[p, h, x * 4 + y, pl.ds(32 * half, 32)]

    def target(h, first, step):
        if (h == 0) == first:
            return (row, place(x0 + step, y0, z0))
        return (row, place(x0, y0 + step, z0))

    def send(p, h, a, b, first, step, k, half=None):
        ref = slab(p, h, a, b, half)
        pltpu.make_async_remote_copy(
            ref, ref, ssem.at[p, h], rsem.at[p, h, k],
            device_id=target(h, first, step), device_id_type=MESH,
        ).start()

    def await_rows(p, h, k, slabs=1):
        ref = lt.at[p, h, pl.ds(0, slabs)]
        pltpu.make_async_copy(ref, ref, rsem.at[p, h, k]).wait()

    def phase1(p):
        ref = lt.at[p, :, 0]
        pltpu.make_async_copy(ref, ref, zsem.at[p]).wait()
        for h in (0, 1):
            send(p, h, 0, 0, True, 1, 1)
            send(p, h, 0, 0, True, 3, 2)
            send(p, h, 0, 0, False, 1, 4)
            send(p, h, 0, 0, False, 3, 5)

    def phase2(p):
        for h in (0, 1):
            await_rows(p, h, 1)
            send(p, h, 3, 0, True, 1, 3, 0)
            send(p, h, 3, 0, False, 1, 7)
            send(p, h, 3, 0, False, 3, 8)
        for h in (0, 1):
            await_rows(p, h, 2)
            send(p, h, 1, 0, True, 3, 3, 1)
            send(p, h, 1, 0, False, 1, 7)
            send(p, h, 1, 0, False, 3, 8)
        for h in (0, 1):
            await_rows(p, h, 4)
            send(p, h, 0, 3, False, 1, 6, 0)
            await_rows(p, h, 5)
            send(p, h, 0, 1, False, 3, 6, 1)

    def phase3(p):
        for h in (0, 1):
            await_rows(p, h, 3)
            send(p, h, 2, 0, False, 1, 10)
            send(p, h, 2, 0, False, 3, 11)
        for h in (0, 1):
            await_rows(p, h, 7, 2)
            send(p, h, 3, 3, False, 1, 9, 0)
            send(p, h, 1, 3, False, 1, 9, 0)
            await_rows(p, h, 8, 2)
            send(p, h, 3, 1, False, 3, 9, 1)
            send(p, h, 1, 1, False, 3, 9, 1)

    def phase4(p):
        for h in (0, 1):
            await_rows(p, h, 10)
            send(p, h, 2, 3, False, 1, 12, 0)
            await_rows(p, h, 11)
            send(p, h, 2, 1, False, 3, 12, 1)

    def finish(p):
        for h in (0, 1):
            await_rows(p, h, 6)
            await_rows(p, h, 9, 2)
            await_rows(p, h, 12)

    def slot_of(k):
        away, side = (k // 2 + zh) % 2, (k % 2 + core) % 2
        return away + PIECES * side, away + side + 3 * (1 - away) * (1 - side) - away * (1 - side)

    def diagonal(slot, k, h):
        return lt[slot, h, pl.ds(4 * k + 2 * h, 2)].reshape(128, 128)

    def invert_pair(slots, rows):
        which = [(s, k, h) for s, k in zip(slots, rows) for h in (0, 1)]
        for (_, k, h), x in zip(which, invert([diagonal(*w) for w in which])):
            xinv[k, h] = x

    def write(b):
        return pltpu.make_async_copy(work.at[b], out.at[b], outsem.at[b])

    def solve():
        for k in range(4):
            slot, index = slot_of(k)
            for h in (0, 1):
                at = 256 * k + 128 * h
                value = bh[index, pl.ds(128 * h, 128), :]
                if at:
                    part = lt[slot, h, pl.ds(0, at // 64)].reshape(at, 128)
                    value = value - product(part, yh[0:at, :], yl[0:at, :])
                answer = dot_t(xinv[k, h], value, HI)
                y[at : at + 128, :] = answer
                high, low = split(answer)
                yh[at : at + 128, :] = high
                yl[at : at + 128, :] = low
        work[0] = y[pl.ds(pl.multiple_of(row * 256, 256), 256), :]

    def trail(p):
        for h in (0, 1):
            rows = pl.ds(128 * h, 128)
            update = product(lt[p, h].reshape(1024, 128), yh[...], yl[...])
            work[p - 1, rows, :] = work[p - 1, rows, :] - update
        write(p - 1).start()

    @pl.loop(0, PIECES + 5)
    def _(t):
        pl.when(t + AHEAD < PIECES)(lambda: scatter_z(t + AHEAD, t + AHEAD - 1))
        pl.when(t < PIECES)(lambda: phase1(t))
        pl.when((t >= 2) & (t < PIECES + 2))(lambda: phase2(t - 2))
        pl.when((t >= 3) & (t < PIECES + 3))(lambda: phase3(t - 3))
        pl.when((t >= 4) & (t < PIECES + 4))(lambda: phase4(t - 4))
        pl.when(t >= 5)(lambda: finish(t - 5))

        pl.when((t >= RIGHT_FROM) & (t < RIGHT_FROM + 4))(
            lambda: half_copy(pl.ds(64 * (t - RIGHT_FROM), 64)).start()
        )

        @pl.when(t == RIGHT_BY)
        def _():
            half_copy(pl.ds(0, 256)).wait()
            last.start()

        @pl.when(t == 6)
        def _():
            for p in (0, 1):
                sibling_head(p).start()

        @pl.when(t == INVERT_OWN)
        def _():
            invert_pair((0, 1), (row, other))

        @pl.when(t == INVERT_SIBLING)
        def _():
            for p in (0, 1):
                sibling_head(p).wait()
            invert_pair((PIECES, PIECES + 1), (sibling, (1 - zh) * 2 + 1 - core))

        @pl.when(t == SOLVE)
        def _():
            core_copy.wait()
            last.wait()
            pltpu.make_async_copy(rhs, work, insem.at[0]).wait()
            pltpu.make_async_copy(rhs.at[0], bh.at[3], insem.at[1]).wait()
            solve()
            write(0).start()

        late = t // (SOLVE + 3)

        @pl.loop(0, 3)
        def _(q):
            p = (1 - late) * (2 + 3 * (t - SOLVE - 1) + q) + late * (t - 5)
            pl.when((t > SOLVE) & (late * q == 0) & (p <= t - 5))(lambda: trail(p))

    @pl.loop(0, PIECES)
    def _(p):
        part = lt.at[p, :, 0, pl.ds(0, 48)]
        pltpu.make_async_copy(part, part, zsend.at[p]).wait()
        for h in (0, 1):
            part = lt.at[p, h, pl.ds(0, 15)]
            pltpu.make_async_copy(part, part, ssem.at[p, h]).wait()

    part = lt.at[1, :, 0, pl.ds(0, 16)]
    pltpu.make_async_copy(part, part, zsend.at[1]).wait()

    @pl.loop(0, 10)
    def _(b):
        write(b).wait()


def substitute(ft, rhs):
    dma = pltpu.SemaphoreType.DMA
    anywhere = pl.BlockSpec(memory_space=pl.ANY)
    return pl.pallas_call(
        kernel,
        out_shape=jax.ShapeDtypeStruct((10, 256, 512), jnp.float32),
        in_specs=[anywhere, anywhere],
        out_specs=anywhere,
        scratch_shapes=[
            pltpu.VMEM((SLOTS, 2, 16, 64, 128), jnp.float32),
            pltpu.VMEM((10, 2, 16, 128), jnp.float32),
            pltpu.VMEM((4, 256, 512), jnp.float32),
            pltpu.VMEM((10, 256, 512), jnp.float32),
            pltpu.VMEM((4, 2, 128, 128), jnp.float32),
            pltpu.VMEM((1024, 512), jnp.float32),
            pltpu.VMEM((1024, 512), jnp.bfloat16),
            pltpu.VMEM((1024, 512), jnp.bfloat16),
            dma((PIECES, 2, 13)), dma((PIECES,)), dma((PIECES,)), dma((PIECES, 2)), dma((2,)),
            dma((3,)), dma((3,)), dma((2,)), dma((2,)), dma((2,)), dma((10,)),
        ],
        compiler_params=pltpu.CompilerParams(
            collective_id=0, has_side_effects=True, vmem_limit_bytes=60 * 1024 * 1024
        ),
        name="substitute",
    )(ft, rhs)


def body(right_sides, factor):
    return substitute(jnp.swapaxes(factor[:, 0], 1, 2), right_sides[:, 0])[:, None]


def solution(mesh):
    placed = (P(None, "row", None, "real"), P(None, "row", None, "real"))
    return jax.shard_map(
        body, mesh=mesh, in_specs=placed, out_specs=P(None, "row", None, "real"), check_vma=False
    )
```

```python
import jax
import jax.numpy as jnp
from jax import lax
from jax.experimental import pallas as pl
from jax.experimental.pallas import tpu as pltpu
from jax.sharding import PartitionSpec as P

MESH = pl.DeviceIdType.MESH
PIECES = 11
SLOTS = 13
AHEAD = 4
RIGHT_FROM, RIGHT_BY = 4, 9
INVERT_OWN, INVERT_SIBLING, SOLVE = 7, 9, 10
HI = lax.Precision.HIGHEST


def dot(a, b, precision=None):
    return jnp.dot(a, b, precision=precision, preferred_element_type=jnp.float32)


def dot_t(a, b, precision=None):
    return lax.dot_general(
        a, b, (((0,), (0,)), ((), ())), precision=precision, preferred_element_type=jnp.float32
    )


def split(value):
    high = value.astype(jnp.bfloat16)
    return high, (value - high.astype(jnp.float32)).astype(jnp.bfloat16)


def product(lt_part, yh, yl):
    high, low = split(lt_part)
    return dot_t(high, yh) + dot_t(high, yl) + dot_t(low, yh)


def invert(uppers):
    r = lax.broadcasted_iota(jnp.int32, (128, 128), 0)
    c = lax.broadcasted_iota(jnp.int32, (128, 128), 1)
    xs = [
        jnp.where(r == c, 1.0 / jnp.sum(jnp.where(r == c, u, 0.0), axis=0, keepdims=True), 0.0)
        for u in uppers
    ]
    size = 1
    while size < 128:
        cross = (c // (2 * size) == r // (2 * size)) & (c // size != r // size) & (c > r)
        inner = [dot(x, jnp.where(cross, u, 0.0), HI) for x, u in zip(xs, uppers)]
        xs = [x - dot(i, x, HI) for x, i in zip(xs, inner)]
        size *= 2
    return xs


def kernel(
    ft, rhs, work, lt, stage, bh, xinv, y, yh, yl,
    rsem, zsem, zsend, ssem, stsem, bsem, bsend, xsem, xsend, insem,
):
    row = lax.axis_index("row")
    real = lax.axis_index("real")
    zh, core = row // 2, row % 2
    x0, y0, z0 = real // 16, (real // 4) % 4, real % 4
    other = (1 - zh) * 2 + core
    sibling = zh * 2 + (1 - core)

    def place(x, y, z):
        return (x % 4) * 16 + (y % 4) * 4 + z

    near = [(row, place(x0 + d, y0, z0)) for d in (1, 3)]
    near += [(row, place(x0, y0 + d, z0)) for d in (1, 3)]
    near += [(row, place(x0, y0, (z0 + d) % 4)) for d in (1, 2, 3)]
    near += [(other, place(x0, y0, z)) for z in range(4)]
    near += [(sibling, real)]
    barrier = pltpu.get_barrier_semaphore()
    pltpu.make_async_copy(rhs, work, insem.at[0]).start()
    pltpu.make_async_copy(rhs.at[0], bh.at[3], insem.at[1]).start()
    for h in (0, 1):
        pltpu.make_async_copy(ft.at[:, :, pl.ds(128 * h, 128)], stage.at[:, h], stsem.at[h]).start()
    for device in near:
        pl.semaphore_signal(barrier, inc=1, device_id=device, device_id_type=MESH)
    for h in (0, 1):
        pltpu.make_async_copy(ft.at[:, :, pl.ds(128 * h, 128)], stage.at[:, h], stsem.at[h]).wait()
    pl.semaphore_wait(barrier, len(near))

    def chunk(p):
        return lt.at[p, :, x0 * 4 + y0, pl.ds(16 * z0, 16)]

    def scatter_z(p, block):
        for h in (0, 1):
            own = ft.at[block, :, pl.ds(128 * h, 128)]
            mine = lt.at[p, h, x0 * 4 + y0, pl.ds(16 * z0, 16)]
            pltpu.make_async_copy(own, mine, zsem.at[p]).start()
        for d in (1, 2, 3):
            pltpu.make_async_remote_copy(
                stage.at[block], chunk(p), zsend.at[p], zsem.at[p],
                device_id=(row, place(x0, y0, (z0 + d) % 4)), device_id_type=MESH,
            ).start()

    def half_copy(rows):
        return pltpu.make_async_remote_copy(
            rhs.at[0, rows], bh.at[0, rows], bsend.at[0], bsem.at[0],
            device_id=(other, real), device_id_type=MESH,
        )

    scatter_z(0, 0)
    for z in range(4):
        pltpu.make_async_remote_copy(
            stage.at[0], chunk(1), zsend.at[1], zsem.at[1],
            device_id=(other, place(x0, y0, z)), device_id_type=MESH,
        ).start()
    for p in range(2, AHEAD):
        scatter_z(p, p - 1)
    core_copy = pltpu.make_async_remote_copy(
        rhs.at[0], bh.at[1], bsend.at[1], bsem.at[1], device_id=(sibling, real), device_id_type=MESH
    )
    core_copy.start()
    last = pltpu.make_async_remote_copy(
        bh.at[0], bh.at[2], bsend.at[2], bsem.at[2], device_id=(sibling, real), device_id_type=MESH
    )

    def sibling_head(p):
        return pltpu.make_async_remote_copy(
            lt.at[p], lt.at[PIECES + p], xsend.at[p], xsem.at[p],
            device_id=(sibling, real), device_id_type=MESH,
        )

    def slab(p, h, a, b, half=None):
        x, y = ((x0 + a) % 4, (y0 + b) % 4) if h == 0 else ((x0 + b) % 4, (y0 + a) % 4)
        if half is None:
            return lt.at[p, h, x * 4 + y]
        return lt.at[p, h, x * 4 + y, pl.ds(32 * half, 32)]

    def target(h, first, step):
        if (h == 0) == first:
            return (row, place(x0 + step, y0, z0))
        return (row, place(x0, y0 + step, z0))

    def send(p, h, a, b, first, step, k, half=None):
        ref = slab(p, h, a, b, half)
        pltpu.make_async_remote_copy(
            ref, ref, ssem.at[p, h], rsem.at[p, h, k],
            device_id=target(h, first, step), device_id_type=MESH,
        ).start()

    def await_rows(p, h, k, slabs=1):
        ref = lt.at[p, h, pl.ds(0, slabs)]
        pltpu.make_async_copy(ref, ref, rsem.at[p, h, k]).wait()

    def phase1(p):
        ref = lt.at[p, :, 0]
        pltpu.make_async_copy(ref, ref, zsem.at[p]).wait()
        for h in (0, 1):
            send(p, h, 0, 0, True, 1, 1)
            send(p, h, 0, 0, True, 3, 2)
            send(p, h, 0, 0, False, 1, 4)
            send(p, h, 0, 0, False, 3, 5)

    def phase2(p):
        for h in (0, 1):
            await_rows(p, h, 1)
            send(p, h, 3, 0, True, 1, 3, 0)
            send(p, h, 3, 0, False, 1, 7)
            send(p, h, 3, 0, False, 3, 8)
        for h in (0, 1):
            await_rows(p, h, 2)
            send(p, h, 1, 0, True, 3, 3, 1)
            send(p, h, 1, 0, False, 1, 7)
            send(p, h, 1, 0, False, 3, 8)
        for h in (0, 1):
            await_rows(p, h, 4)
            send(p, h, 0, 3, False, 1, 6, 0)
            await_rows(p, h, 5)
            send(p, h, 0, 1, False, 3, 6, 1)

    def phase3(p):
        for h in (0, 1):
            await_rows(p, h, 3)
            send(p, h, 2, 0, False, 1, 10)
            send(p, h, 2, 0, False, 3, 11)
        for h in (0, 1):
            await_rows(p, h, 7, 2)
            send(p, h, 3, 3, False, 1, 9, 0)
            send(p, h, 1, 3, False, 1, 9, 0)
            await_rows(p, h, 8, 2)
            send(p, h, 3, 1, False, 3, 9, 1)
            send(p, h, 1, 1, False, 3, 9, 1)

    def phase4(p):
        for h in (0, 1):
            await_rows(p, h, 10)
            send(p, h, 2, 3, False, 1, 12, 0)
            await_rows(p, h, 11)
            send(p, h, 2, 1, False, 3, 12, 1)

    def finish(p):
        for h in (0, 1):
            await_rows(p, h, 6)
            await_rows(p, h, 9, 2)
            await_rows(p, h, 12)

    def slot_of(k):
        away, side = (k // 2 + zh) % 2, (k % 2 + core) % 2
        return away + PIECES * side, away + side + 3 * (1 - away) * (1 - side) - away * (1 - side)

    def diagonal(slot, k, h):
        return lt[slot, h, pl.ds(4 * k + 2 * h, 2)].reshape(128, 128)

    def invert_pair(slots, rows):
        which = [(s, k, h) for s, k in zip(slots, rows) for h in (0, 1)]
        for (_, k, h), x in zip(which, invert([diagonal(*w) for w in which])):
            xinv[k, h] = x

    def solve():
        for k in range(4):
            slot, index = slot_of(k)
            for h in (0, 1):
                at = 256 * k + 128 * h
                value = bh[index, pl.ds(128 * h, 128), :]
                if at:
                    part = lt[slot, h, pl.ds(0, at // 64)].reshape(at, 128)
                    value = value - product(part, yh[0:at, :], yl[0:at, :])
                answer = dot_t(xinv[k, h], value, HI)
                y[at : at + 128, :] = answer
                high, low = split(answer)
                yh[at : at + 128, :] = high
                yl[at : at + 128, :] = low
        work[0] = y[pl.ds(pl.multiple_of(row * 256, 256), 256), :]

    def trail(p):
        for h in (0, 1):
            rows = pl.ds(128 * h, 128)
            update = product(lt[p, h].reshape(1024, 128), yh[...], yl[...])
            work[p - 1, rows, :] = work[p - 1, rows, :] - update

    @pl.loop(0, PIECES + 5)
    def _(t):
        pl.when(t + AHEAD < PIECES)(lambda: scatter_z(t + AHEAD, t + AHEAD - 1))
        pl.when(t < PIECES)(lambda: phase1(t))
        pl.when((t >= 2) & (t < PIECES + 2))(lambda: phase2(t - 2))
        pl.when((t >= 3) & (t < PIECES + 3))(lambda: phase3(t - 3))
        pl.when((t >= 4) & (t < PIECES + 4))(lambda: phase4(t - 4))
        pl.when(t >= 5)(lambda: finish(t - 5))

        pl.when((t >= RIGHT_FROM) & (t < RIGHT_FROM + 4))(
            lambda: half_copy(pl.ds(64 * (t - RIGHT_FROM), 64)).start()
        )

        @pl.when(t == RIGHT_BY)
        def _():
            half_copy(pl.ds(0, 256)).wait()
            last.start()

        @pl.when(t == 6)
        def _():
            for p in (0, 1):
                sibling_head(p).start()

        @pl.when(t == INVERT_OWN)
        def _():
            invert_pair((0, 1), (row, other))

        @pl.when(t == INVERT_SIBLING)
        def _():
            for p in (0, 1):
                sibling_head(p).wait()
            invert_pair((PIECES, PIECES + 1), (sibling, (1 - zh) * 2 + 1 - core))

        @pl.when(t == SOLVE)
        def _():
            core_copy.wait()
            last.wait()
            pltpu.make_async_copy(rhs, work, insem.at[0]).wait()
            pltpu.make_async_copy(rhs.at[0], bh.at[3], insem.at[1]).wait()
            solve()

        late = t // (SOLVE + 3)

        @pl.loop(0, 3)
        def _(q):
            p = (1 - late) * (2 + 3 * (t - SOLVE - 1) + q) + late * (t - 5)
            pl.when((t > SOLVE) & (late * q == 0) & (p <= t - 5))(lambda: trail(p))

    @pl.loop(0, PIECES)
    def _(p):
        part = lt.at[p, :, 0, pl.ds(0, 48)]
        pltpu.make_async_copy(part, part, zsend.at[p]).wait()
        for h in (0, 1):
            part = lt.at[p, h, pl.ds(0, 15)]
            pltpu.make_async_copy(part, part, ssem.at[p, h]).wait()

    part = lt.at[1, :, 0, pl.ds(0, 16)]
    pltpu.make_async_copy(part, part, zsend.at[1]).wait()


def substitute(ft, rhs):
    dma = pltpu.SemaphoreType.DMA
    hbm = pl.BlockSpec(memory_space=pltpu.HBM)
    return pl.pallas_call(
        kernel,
        out_shape=pltpu.VMEM((10, 256, 512), jnp.float32),
        in_specs=[hbm, hbm],
        out_specs=pl.BlockSpec(memory_space=pltpu.VMEM),
        scratch_shapes=[
            pltpu.VMEM((SLOTS, 2, 16, 64, 128), jnp.float32),
            pltpu.VMEM((10, 2, 16, 128), jnp.float32),
            pltpu.VMEM((4, 256, 512), jnp.float32),
            pltpu.VMEM((4, 2, 128, 128), jnp.float32),
            pltpu.VMEM((1024, 512), jnp.float32),
            pltpu.VMEM((1024, 512), jnp.bfloat16),
            pltpu.VMEM((1024, 512), jnp.bfloat16),
            dma((PIECES, 2, 13)), dma((PIECES,)), dma((PIECES,)), dma((PIECES, 2)), dma((2,)),
            dma((3,)), dma((3,)), dma((2,)), dma((2,)), dma((2,)),
        ],
        compiler_params=pltpu.CompilerParams(
            collective_id=0, has_side_effects=True, vmem_limit_bytes=36 * 1024 * 1024
        ),
        name="substitute",
    )(ft, rhs)


def body(right_sides, factor):
    ft = pltpu.with_memory_space_constraint(jnp.swapaxes(factor[:, 0], 1, 2), pltpu.HBM)
    rhs = pltpu.with_memory_space_constraint(right_sides[:, 0], pltpu.HBM)
    return substitute(ft, rhs)[:, None]


def solution(mesh):
    placed = (P(None, "row", None, "real"), P(None, "row", None, "real"))
    return jax.shard_map(
        body, mesh=mesh, in_specs=placed, out_specs=P(None, "row", None, "real"), check_vma=False
    )
```

```python
import jax
import jax.numpy as jnp
from jax import lax
from jax.experimental import pallas as pl
from jax.experimental.pallas import tpu as pltpu
from jax.sharding import PartitionSpec as P

MESH = pl.DeviceIdType.MESH
PIECES = 11
SLOTS = 13
AHEAD = 4
RIGHT_FROM, RIGHT_BY = 4, 9
INVERT_OWN, INVERT_SIBLING, SOLVE = 6, 8, 10
HI = lax.Precision.HIGHEST


def dot(a, b, precision=None):
    return jnp.dot(a, b, precision=precision, preferred_element_type=jnp.float32)


def dot_t(a, b, precision=None):
    return lax.dot_general(
        a, b, (((0,), (0,)), ((), ())), precision=precision, preferred_element_type=jnp.float32
    )


def split(value):
    high = value.astype(jnp.bfloat16)
    return high, (value - high.astype(jnp.float32)).astype(jnp.bfloat16)


def product(lt_part, yh, yl):
    high, low = split(lt_part)
    return dot_t(high, yh) + dot_t(high, yl) + dot_t(low, yh)


def invert(uppers):
    r = lax.broadcasted_iota(jnp.int32, (128, 128), 0)
    c = lax.broadcasted_iota(jnp.int32, (128, 128), 1)
    xs = [
        jnp.where(r == c, 1.0 / jnp.sum(jnp.where(r == c, u, 0.0), axis=0, keepdims=True), 0.0)
        for u in uppers
    ]
    size = 1
    while size < 128:
        cross = (c // (2 * size) == r // (2 * size)) & (c // size != r // size) & (c > r)
        inner = [dot(x, jnp.where(cross, u, 0.0), HI) for x, u in zip(xs, uppers)]
        xs = [x - dot(i, x, HI) for x, i in zip(xs, inner)]
        size *= 2
    return xs


def kernel(
    ft, rhs, work, lt, stage, bh, xinv, y, yh, yl,
    rsem, zsem, zsend, ssem, stsem, bsem, bsend, xsem, xsend, insem,
):
    row = lax.axis_index("row")
    real = lax.axis_index("real")
    zh, core = row // 2, row % 2
    x0, y0, z0 = real // 16, (real // 4) % 4, real % 4
    other = (1 - zh) * 2 + core
    sibling = zh * 2 + (1 - core)

    def place(x, y, z):
        return (x % 4) * 16 + (y % 4) * 4 + z

    near = [(row, place(x0 + d, y0, z0)) for d in (1, 3)]
    near += [(row, place(x0, y0 + d, z0)) for d in (1, 3)]
    near += [(row, place(x0, y0, (z0 + d) % 4)) for d in (1, 2, 3)]
    near += [(other, place(x0, y0, z)) for z in range(4)]
    near += [(sibling, real)]
    barrier = pltpu.get_barrier_semaphore()
    pltpu.make_async_copy(rhs, work, insem.at[0]).start()
    pltpu.make_async_copy(rhs.at[0], bh.at[3], insem.at[1]).start()
    for h in (0, 1):
        pltpu.make_async_copy(ft.at[:, :, pl.ds(128 * h, 128)], stage.at[:, h], stsem.at[h]).start()
    for device in near:
        pl.semaphore_signal(barrier, inc=1, device_id=device, device_id_type=MESH)
    for h in (0, 1):
        pltpu.make_async_copy(ft.at[:, :, pl.ds(128 * h, 128)], stage.at[:, h], stsem.at[h]).wait()
    pl.semaphore_wait(barrier, len(near))

    def chunk(p):
        return lt.at[p, :, x0 * 4 + y0, pl.ds(16 * z0, 16)]

    def scatter_z(p, block):
        for h in (0, 1):
            own = ft.at[block, :, pl.ds(128 * h, 128)]
            mine = lt.at[p, h, x0 * 4 + y0, pl.ds(16 * z0, 16)]
            pltpu.make_async_copy(own, mine, zsem.at[p]).start()
        for d in (1, 2, 3):
            pltpu.make_async_remote_copy(
                stage.at[block], chunk(p), zsend.at[p], zsem.at[p],
                device_id=(row, place(x0, y0, (z0 + d) % 4)), device_id_type=MESH,
            ).start()

    def half_copy(rows):
        return pltpu.make_async_remote_copy(
            rhs.at[0, rows], bh.at[0, rows], bsend.at[0], bsem.at[0],
            device_id=(other, real), device_id_type=MESH,
        )

    scatter_z(0, 0)
    for z in range(4):
        pltpu.make_async_remote_copy(
            stage.at[0], chunk(1), zsend.at[1], zsem.at[1],
            device_id=(other, place(x0, y0, z)), device_id_type=MESH,
        ).start()
    for p in range(2, AHEAD):
        scatter_z(p, p - 1)
    core_copy = pltpu.make_async_remote_copy(
        rhs.at[0], bh.at[1], bsend.at[1], bsem.at[1], device_id=(sibling, real), device_id_type=MESH
    )
    core_copy.start()
    last = pltpu.make_async_remote_copy(
        bh.at[0], bh.at[2], bsend.at[2], bsem.at[2], device_id=(sibling, real), device_id_type=MESH
    )

    def sibling_head(p):
        return pltpu.make_async_remote_copy(
            lt.at[p], lt.at[PIECES + p], xsend.at[p], xsem.at[p],
            device_id=(sibling, real), device_id_type=MESH,
        )

    def slab(p, h, a, b, half=None):
        x, y = ((x0 + a) % 4, (y0 + b) % 4) if h == 0 else ((x0 + b) % 4, (y0 + a) % 4)
        if half is None:
            return lt.at[p, h, x * 4 + y]
        return lt.at[p, h, x * 4 + y, pl.ds(32 * half, 32)]

    def target(h, first, step):
        if (h == 0) == first:
            return (row, place(x0 + step, y0, z0))
        return (row, place(x0, y0 + step, z0))

    def send(p, h, a, b, first, step, k, half=None):
        ref = slab(p, h, a, b, half)
        pltpu.make_async_remote_copy(
            ref, ref, ssem.at[p, h], rsem.at[p, h, k],
            device_id=target(h, first, step), device_id_type=MESH,
        ).start()

    def await_rows(p, h, k, slabs=1):
        ref = lt.at[p, h, pl.ds(0, slabs)]
        pltpu.make_async_copy(ref, ref, rsem.at[p, h, k]).wait()

    def phase1(p):
        ref = lt.at[p, :, 0]
        pltpu.make_async_copy(ref, ref, zsem.at[p]).wait()
        for h in (0, 1):
            send(p, h, 0, 0, True, 1, 1)
            send(p, h, 0, 0, True, 3, 2)
            send(p, h, 0, 0, False, 1, 4)
            send(p, h, 0, 0, False, 3, 5)

    def phase2(p):
        for h in (0, 1):
            await_rows(p, h, 1)
            send(p, h, 3, 0, True, 1, 3, 0)
            send(p, h, 3, 0, False, 1, 7)
            send(p, h, 3, 0, False, 3, 8)
        for h in (0, 1):
            await_rows(p, h, 2)
            send(p, h, 1, 0, True, 3, 3, 1)
            send(p, h, 1, 0, False, 1, 7)
            send(p, h, 1, 0, False, 3, 8)
        for h in (0, 1):
            await_rows(p, h, 4)
            send(p, h, 0, 3, False, 1, 6, 0)
            await_rows(p, h, 5)
            send(p, h, 0, 1, False, 3, 6, 1)

    def phase3(p):
        for h in (0, 1):
            await_rows(p, h, 3)
            send(p, h, 2, 0, False, 1, 10)
            send(p, h, 2, 0, False, 3, 11)
        for h in (0, 1):
            await_rows(p, h, 7, 2)
            send(p, h, 3, 3, False, 1, 9, 0)
            send(p, h, 1, 3, False, 1, 9, 0)
            await_rows(p, h, 8, 2)
            send(p, h, 3, 1, False, 3, 9, 1)
            send(p, h, 1, 1, False, 3, 9, 1)

    def phase4(p):
        for h in (0, 1):
            await_rows(p, h, 10)
            send(p, h, 2, 3, False, 1, 12, 0)
            await_rows(p, h, 11)
            send(p, h, 2, 1, False, 3, 12, 1)

    def finish(p):
        for h in (0, 1):
            await_rows(p, h, 6)
            await_rows(p, h, 9, 2)
            await_rows(p, h, 12)

    def slot_of(k):
        away, side = (k // 2 + zh) % 2, (k % 2 + core) % 2
        return away + PIECES * side, away + side + 3 * (1 - away) * (1 - side) - away * (1 - side)

    def diagonal(slot, k, h):
        return lt[slot, h, pl.ds(4 * k + 2 * h, 2)].reshape(128, 128)

    def invert_pair(slots, rows):
        which = [(s, k, h) for s, k in zip(slots, rows) for h in (0, 1)]
        for (_, k, h), x in zip(which, invert([diagonal(*w) for w in which])):
            xinv[k, h] = x

    def solve():
        for k in range(4):
            slot, index = slot_of(k)
            for h in (0, 1):
                at = 256 * k + 128 * h
                value = bh[index, pl.ds(128 * h, 128), :]
                if at:
                    part = lt[slot, h, pl.ds(0, at // 64)].reshape(at, 128)
                    value = value - product(part, yh[0:at, :], yl[0:at, :])
                answer = dot_t(xinv[k, h], value, HI)
                y[at : at + 128, :] = answer
                high, low = split(answer)
                yh[at : at + 128, :] = high
                yl[at : at + 128, :] = low
        work[0] = y[pl.ds(pl.multiple_of(row * 256, 256), 256), :]

    def trail(p):
        for h in (0, 1):
            rows = pl.ds(128 * h, 128)
            update = product(lt[p, h].reshape(1024, 128), yh[...], yl[...])
            work[p - 1, rows, :] = work[p - 1, rows, :] - update

    @pl.loop(0, PIECES + 5)
    def _(t):
        pl.when(t + AHEAD < PIECES)(lambda: scatter_z(t + AHEAD, t + AHEAD - 1))
        pl.when(t < PIECES)(lambda: phase1(t))
        pl.when((t >= 2) & (t < PIECES + 2))(lambda: phase2(t - 2))
        pl.when((t >= 3) & (t < PIECES + 3))(lambda: phase3(t - 3))
        pl.when((t >= 4) & (t < PIECES + 4))(lambda: phase4(t - 4))
        pl.when(t >= 5)(lambda: finish(t - 5))

        pl.when((t >= RIGHT_FROM) & (t < RIGHT_FROM + 4))(
            lambda: half_copy(pl.ds(64 * (t - RIGHT_FROM), 64)).start()
        )

        @pl.when(t == RIGHT_BY)
        def _():
            half_copy(pl.ds(0, 256)).wait()
            last.start()

        @pl.when(t == 6)
        def _():
            for p in (0, 1):
                sibling_head(p).start()

        @pl.when(t == INVERT_OWN)
        def _():
            invert_pair((0, 1), (row, other))

        @pl.when(t == INVERT_SIBLING)
        def _():
            for p in (0, 1):
                sibling_head(p).wait()
            invert_pair((PIECES, PIECES + 1), (sibling, (1 - zh) * 2 + 1 - core))

        @pl.when(t == SOLVE)
        def _():
            core_copy.wait()
            last.wait()
            pltpu.make_async_copy(rhs, work, insem.at[0]).wait()
            pltpu.make_async_copy(rhs.at[0], bh.at[3], insem.at[1]).wait()
            solve()

        late = t // (SOLVE + 3)

        @pl.loop(0, 3)
        def _(q):
            p = (1 - late) * (2 + 3 * (t - SOLVE - 1) + q) + late * (t - 5)
            pl.when((t > SOLVE) & (late * q == 0) & (p <= t - 5))(lambda: trail(p))

    @pl.loop(0, PIECES)
    def _(p):
        part = lt.at[p, :, 0, pl.ds(0, 48)]
        pltpu.make_async_copy(part, part, zsend.at[p]).wait()
        for h in (0, 1):
            part = lt.at[p, h, pl.ds(0, 15)]
            pltpu.make_async_copy(part, part, ssem.at[p, h]).wait()

    part = lt.at[1, :, 0, pl.ds(0, 16)]
    pltpu.make_async_copy(part, part, zsend.at[1]).wait()


def substitute(ft, rhs):
    dma = pltpu.SemaphoreType.DMA
    hbm = pl.BlockSpec(memory_space=pltpu.HBM)
    return pl.pallas_call(
        kernel,
        out_shape=pltpu.VMEM((10, 256, 512), jnp.float32),
        in_specs=[hbm, hbm],
        out_specs=pl.BlockSpec(memory_space=pltpu.VMEM),
        scratch_shapes=[
            pltpu.VMEM((SLOTS, 2, 16, 64, 128), jnp.float32),
            pltpu.VMEM((10, 2, 16, 128), jnp.float32),
            pltpu.VMEM((4, 256, 512), jnp.float32),
            pltpu.VMEM((4, 2, 128, 128), jnp.float32),
            pltpu.VMEM((1024, 512), jnp.float32),
            pltpu.VMEM((1024, 512), jnp.bfloat16),
            pltpu.VMEM((1024, 512), jnp.bfloat16),
            dma((PIECES, 2, 13)), dma((PIECES,)), dma((PIECES,)), dma((PIECES, 2)), dma((2,)),
            dma((3,)), dma((3,)), dma((2,)), dma((2,)), dma((2,)),
        ],
        compiler_params=pltpu.CompilerParams(
            collective_id=0, has_side_effects=True, vmem_limit_bytes=36 * 1024 * 1024
        ),
        name="substitute",
    )(ft, rhs)


def body(right_sides, factor):
    ft = pltpu.with_memory_space_constraint(jnp.swapaxes(factor[:, 0], 1, 2), pltpu.HBM)
    rhs = pltpu.with_memory_space_constraint(right_sides[:, 0], pltpu.HBM)
    return substitute(ft, rhs)[:, None]


def solution(mesh):
    placed = (P(None, "row", None, "real"), P(None, "row", None, "real"))
    return jax.shard_map(
        body, mesh=mesh, in_specs=placed, out_specs=P(None, "row", None, "real"), check_vma=False
    )
```

```python
import jax
import jax.numpy as jnp
from jax import lax
from jax.experimental import pallas as pl
from jax.experimental.pallas import tpu as pltpu
from jax.sharding import PartitionSpec as P

MESH = pl.DeviceIdType.MESH
PIECES = 11
SLOTS = 13
AHEAD = 4
RIGHT_AT, RIGHT_BY = (2, 4, 6, 7), 9
INVERT_OWN, INVERT_SIBLING, SOLVE = 6, 8, 10
HI = lax.Precision.HIGHEST


def dot(a, b, precision=None):
    return jnp.dot(a, b, precision=precision, preferred_element_type=jnp.float32)


def dot_t(a, b, precision=None):
    return lax.dot_general(
        a, b, (((0,), (0,)), ((), ())), precision=precision, preferred_element_type=jnp.float32
    )


def split(value):
    high = value.astype(jnp.bfloat16)
    return high, (value - high.astype(jnp.float32)).astype(jnp.bfloat16)


def product(lt_part, yh, yl):
    high, low = split(lt_part)
    return dot_t(high, yh) + dot_t(high, yl) + dot_t(low, yh)


def invert(uppers):
    r = lax.broadcasted_iota(jnp.int32, (128, 128), 0)
    c = lax.broadcasted_iota(jnp.int32, (128, 128), 1)
    xs = [
        jnp.where(r == c, 1.0 / jnp.sum(jnp.where(r == c, u, 0.0), axis=0, keepdims=True), 0.0)
        for u in uppers
    ]
    size = 1
    while size < 128:
        cross = (c // (2 * size) == r // (2 * size)) & (c // size != r // size) & (c > r)
        inner = [dot(x, jnp.where(cross, u, 0.0), HI) for x, u in zip(xs, uppers)]
        xs = [x - dot(i, x, HI) for x, i in zip(xs, inner)]
        size *= 2
    return xs


def kernel(
    ft, rhs, work, lt, stage, bh, xinv, y, yh, yl,
    rsem, zsem, zsend, ssem, stsem, bsem, bsend, xsem, xsend, insem, relay, rsend, rrecv,
):
    row = lax.axis_index("row")
    real = lax.axis_index("real")
    zh, core = row // 2, row % 2
    x0, y0, z0 = real // 16, (real // 4) % 4, real % 4
    other = (1 - zh) * 2 + core
    sibling = zh * 2 + (1 - core)

    def place(x, y, z):
        return (x % 4) * 16 + (y % 4) * 4 + z

    near = [(row, place(x0 + d, y0, z0)) for d in (1, 3)]
    near += [(row, place(x0, y0 + d, z0)) for d in (1, 3)]
    near += [(row, place(x0, y0, (z0 + d) % 4)) for d in (1, 2, 3)]
    near += [(other, place(x0, y0, z)) for z in range(4)]
    near += [(sibling, real)]
    barrier = pltpu.get_barrier_semaphore()
    pltpu.make_async_copy(rhs, work, insem.at[0]).start()
    pltpu.make_async_copy(rhs.at[0], bh.at[3], insem.at[1]).start()
    for h in (0, 1):
        pltpu.make_async_copy(ft.at[:, :, pl.ds(128 * h, 128)], stage.at[:, h], stsem.at[h]).start()
    for device in near:
        pl.semaphore_signal(barrier, inc=1, device_id=device, device_id_type=MESH)
    for h in (0, 1):
        pltpu.make_async_copy(ft.at[:, :, pl.ds(128 * h, 128)], stage.at[:, h], stsem.at[h]).wait()
    pl.semaphore_wait(barrier, len(near))

    def chunk(p):
        return lt.at[p, :, x0 * 4 + y0, pl.ds(16 * z0, 16)]

    def scatter_z(p, block):
        for h in (0, 1):
            own = ft.at[block, :, pl.ds(128 * h, 128)]
            mine = lt.at[p, h, x0 * 4 + y0, pl.ds(16 * z0, 16)]
            pltpu.make_async_copy(own, mine, zsem.at[p]).start()
        for d in (1, 2, 3):
            pltpu.make_async_remote_copy(
                stage.at[block], chunk(p), zsend.at[p], zsem.at[p],
                device_id=(row, place(x0, y0, (z0 + d) % 4)), device_id_type=MESH,
            ).start()

    def pass_on(way, step):
        rows = pl.ds(128 * way, 128)
        chip = (zh * 4 + z0 + (1, 7)[way]) % 8
        source = rhs.at[0, rows] if step == 0 else relay.at[way, step - 1]
        into = bh.at[0, rows] if step == 3 else relay.at[way, step]
        return pltpu.make_async_remote_copy(
            source, into, rsend.at[way, step], rrecv.at[way, step],
            device_id=(chip // 4 * 2 + core, place(x0, y0, chip % 4)), device_id_type=MESH,
        )

    scatter_z(0, 0)
    for z in range(4):
        pltpu.make_async_remote_copy(
            stage.at[0], chunk(1), zsend.at[1], zsem.at[1],
            device_id=(other, place(x0, y0, z)), device_id_type=MESH,
        ).start()
    for p in range(2, AHEAD):
        scatter_z(p, p - 1)
    core_copy = pltpu.make_async_remote_copy(
        rhs.at[0], bh.at[1], bsend.at[1], bsem.at[1], device_id=(sibling, real), device_id_type=MESH
    )
    core_copy.start()
    last = pltpu.make_async_remote_copy(
        bh.at[0], bh.at[2], bsend.at[2], bsem.at[2], device_id=(sibling, real), device_id_type=MESH
    )

    def sibling_head(p):
        return pltpu.make_async_remote_copy(
            lt.at[p], lt.at[PIECES + p], xsend.at[p], xsem.at[p],
            device_id=(sibling, real), device_id_type=MESH,
        )

    def slab(p, h, a, b, half=None):
        x, y = ((x0 + a) % 4, (y0 + b) % 4) if h == 0 else ((x0 + b) % 4, (y0 + a) % 4)
        if half is None:
            return lt.at[p, h, x * 4 + y]
        return lt.at[p, h, x * 4 + y, pl.ds(32 * half, 32)]

    def target(h, first, step):
        if (h == 0) == first:
            return (row, place(x0 + step, y0, z0))
        return (row, place(x0, y0 + step, z0))

    def send(p, h, a, b, first, step, k, half=None):
        ref = slab(p, h, a, b, half)
        pltpu.make_async_remote_copy(
            ref, ref, ssem.at[p, h], rsem.at[p, h, k],
            device_id=target(h, first, step), device_id_type=MESH,
        ).start()

    def await_rows(p, h, k, slabs=1):
        ref = lt.at[p, h, pl.ds(0, slabs)]
        pltpu.make_async_copy(ref, ref, rsem.at[p, h, k]).wait()

    def phase1(p):
        ref = lt.at[p, :, 0]
        pltpu.make_async_copy(ref, ref, zsem.at[p]).wait()
        for h in (0, 1):
            send(p, h, 0, 0, True, 1, 1)
            send(p, h, 0, 0, True, 3, 2)
            send(p, h, 0, 0, False, 1, 4)
            send(p, h, 0, 0, False, 3, 5)

    def phase2(p):
        for h in (0, 1):
            await_rows(p, h, 1)
            send(p, h, 3, 0, True, 1, 3, 0)
            send(p, h, 3, 0, False, 1, 7)
            send(p, h, 3, 0, False, 3, 8)
        for h in (0, 1):
            await_rows(p, h, 2)
            send(p, h, 1, 0, True, 3, 3, 1)
            send(p, h, 1, 0, False, 1, 7)
            send(p, h, 1, 0, False, 3, 8)
        for h in (0, 1):
            await_rows(p, h, 4)
            send(p, h, 0, 3, False, 1, 6, 0)
            await_rows(p, h, 5)
            send(p, h, 0, 1, False, 3, 6, 1)

    def phase3(p):
        for h in (0, 1):
            await_rows(p, h, 3)
            send(p, h, 2, 0, False, 1, 10)
            send(p, h, 2, 0, False, 3, 11)
        for h in (0, 1):
            await_rows(p, h, 7, 2)
            send(p, h, 3, 3, False, 1, 9, 0)
            send(p, h, 1, 3, False, 1, 9, 0)
            await_rows(p, h, 8, 2)
            send(p, h, 3, 1, False, 3, 9, 1)
            send(p, h, 1, 1, False, 3, 9, 1)

    def phase4(p):
        for h in (0, 1):
            await_rows(p, h, 10)
            send(p, h, 2, 3, False, 1, 12, 0)
            await_rows(p, h, 11)
            send(p, h, 2, 1, False, 3, 12, 1)

    def finish(p):
        for h in (0, 1):
            await_rows(p, h, 6)
            await_rows(p, h, 9, 2)
            await_rows(p, h, 12)

    def slot_of(k):
        away, side = (k // 2 + zh) % 2, (k % 2 + core) % 2
        return away + PIECES * side, away + side + 3 * (1 - away) * (1 - side) - away * (1 - side)

    def diagonal(slot, k, h):
        return lt[slot, h, pl.ds(4 * k + 2 * h, 2)].reshape(128, 128)

    def invert_pair(slots, rows):
        which = [(s, k, h) for s, k in zip(slots, rows) for h in (0, 1)]
        for (_, k, h), x in zip(which, invert([diagonal(*w) for w in which])):
            xinv[k, h] = x

    def solve():
        for k in range(4):
            slot, index = slot_of(k)
            for h in (0, 1):
                at = 256 * k + 128 * h
                value = bh[index, pl.ds(128 * h, 128), :]
                if at:
                    part = lt[slot, h, pl.ds(0, at // 64)].reshape(at, 128)
                    value = value - product(part, yh[0:at, :], yl[0:at, :])
                answer = dot_t(xinv[k, h], value, HI)
                y[at : at + 128, :] = answer
                high, low = split(answer)
                yh[at : at + 128, :] = high
                yl[at : at + 128, :] = low
        work[0] = y[pl.ds(pl.multiple_of(row * 256, 256), 256), :]

    def trail(p):
        for h in (0, 1):
            rows = pl.ds(128 * h, 128)
            update = product(lt[p, h].reshape(1024, 128), yh[...], yl[...])
            work[p - 1, rows, :] = work[p - 1, rows, :] - update

    @pl.loop(0, PIECES + 5)
    def _(t):
        pl.when(t + AHEAD < PIECES)(lambda: scatter_z(t + AHEAD, t + AHEAD - 1))
        pl.when(t < PIECES)(lambda: phase1(t))
        pl.when((t >= 2) & (t < PIECES + 2))(lambda: phase2(t - 2))
        pl.when((t >= 3) & (t < PIECES + 3))(lambda: phase3(t - 3))
        pl.when((t >= 4) & (t < PIECES + 4))(lambda: phase4(t - 4))
        pl.when(t >= 5)(lambda: finish(t - 5))

        for step, when in enumerate(RIGHT_AT):

            @pl.when(t == when)
            def _(step=step):
                for way in (0, 1):
                    if step:
                        pass_on(way, step - 1).wait_recv()
                    pass_on(way, step).start()

        @pl.when(t == RIGHT_BY)
        def _():
            for way in (0, 1):
                pass_on(way, 3).wait_recv()
            last.start()

        @pl.when(t == 6)
        def _():
            for p in (0, 1):
                sibling_head(p).start()

        @pl.when(t == INVERT_OWN)
        def _():
            invert_pair((0, 1), (row, other))

        @pl.when(t == INVERT_SIBLING)
        def _():
            for p in (0, 1):
                sibling_head(p).wait()
            invert_pair((PIECES, PIECES + 1), (sibling, (1 - zh) * 2 + 1 - core))

        @pl.when(t == SOLVE)
        def _():
            core_copy.wait()
            last.wait()
            pltpu.make_async_copy(rhs, work, insem.at[0]).wait()
            pltpu.make_async_copy(rhs.at[0], bh.at[3], insem.at[1]).wait()
            solve()

        late = t // (SOLVE + 3)

        @pl.loop(0, 3)
        def _(q):
            p = (1 - late) * (2 + 3 * (t - SOLVE - 1) + q) + late * (t - 5)
            pl.when((t > SOLVE) & (late * q == 0) & (p <= t - 5))(lambda: trail(p))

    for way in (0, 1):
        for step in range(4):
            pass_on(way, step).wait_send()

    @pl.loop(0, PIECES)
    def _(p):
        part = lt.at[p, :, 0, pl.ds(0, 48)]
        pltpu.make_async_copy(part, part, zsend.at[p]).wait()
        for h in (0, 1):
            part = lt.at[p, h, pl.ds(0, 15)]
            pltpu.make_async_copy(part, part, ssem.at[p, h]).wait()

    part = lt.at[1, :, 0, pl.ds(0, 16)]
    pltpu.make_async_copy(part, part, zsend.at[1]).wait()


def substitute(ft, rhs):
    dma = pltpu.SemaphoreType.DMA
    hbm = pl.BlockSpec(memory_space=pltpu.HBM)
    return pl.pallas_call(
        kernel,
        out_shape=pltpu.VMEM((10, 256, 512), jnp.float32),
        in_specs=[hbm, hbm],
        out_specs=pl.BlockSpec(memory_space=pltpu.VMEM),
        scratch_shapes=[
            pltpu.VMEM((SLOTS, 2, 16, 64, 128), jnp.float32),
            pltpu.VMEM((10, 2, 16, 128), jnp.float32),
            pltpu.VMEM((4, 256, 512), jnp.float32),
            pltpu.VMEM((4, 2, 128, 128), jnp.float32),
            pltpu.VMEM((1024, 512), jnp.float32),
            pltpu.VMEM((1024, 512), jnp.bfloat16),
            pltpu.VMEM((1024, 512), jnp.bfloat16),
            dma((PIECES, 2, 13)), dma((PIECES,)), dma((PIECES,)), dma((PIECES, 2)), dma((2,)),
            dma((3,)), dma((3,)), dma((2,)), dma((2,)), dma((2,)),
            pltpu.VMEM((2, 3, 128, 512), jnp.float32), dma((2, 4)), dma((2, 4)),
        ],
        compiler_params=pltpu.CompilerParams(
            collective_id=0, has_side_effects=True, vmem_limit_bytes=36 * 1024 * 1024
        ),
        name="substitute",
    )(ft, rhs)


def body(right_sides, factor):
    ft = pltpu.with_memory_space_constraint(jnp.swapaxes(factor[:, 0], 1, 2), pltpu.HBM)
    rhs = pltpu.with_memory_space_constraint(right_sides[:, 0], pltpu.HBM)
    return substitute(ft, rhs)[:, None]


def solution(mesh):
    placed = (P(None, "row", None, "real"), P(None, "row", None, "real"))
    return jax.shard_map(
        body, mesh=mesh, in_specs=placed, out_specs=P(None, "row", None, "real"), check_vma=False
    )
```
